32 devices in a mesh: section: 2 (over core), seq: 16 (over z, y, x).
Axes of the slice: x: 2, y: 2, z: 4, core: 2. Of those that a mesh axis runs over, the one named last changes fastest.
Arguments:
- tokens: bfloat16 [1, 2048, 1024], P(None, 'seq'), may hold values from -24 to 24
- neighbor_ids: int32 [16, 9], P('seq'), may hold values from 0 to 15, as said below
- neighbor_count: int32 [16], P('seq'), may hold values from 1 to 9, as said below
- w_query: bfloat16 [2, 1024, 1024], P('section')
- w_key: bfloat16 [2, 1024, 1024], P('section')
- w_value: bfloat16 [2, 1024, 1024], P('section'), may hold values from -0.1875 to 0.1875
- w_out: bfloat16 [2, 1024, 1024], P('section'), may hold values from -0.1875 to 0.1875
- norm_gain: float32 [2, 1024], P('section'), may hold values from 0.5 to 3
- w_up: bfloat16 [2, 4096, 1024], P('section', 'seq'), may hold values from -0.1875 to 0.1875
- w_down: bfloat16 [2, 4096, 1024], P('section', 'seq'), may hold values from -0.09375 to 0.09375
- mlp_gain: float32 [2, 1024], P('section'), may hold values from 0.5 to 2
Outputs:
- layer_outputs: bfloat16 [2, 1, 2048, 1024], P('section', None, 'seq')
The draws below stay inside these ranges and needn't reach their ends.
Inputs may be any that keep to these rules, and one draw needn't show every extreme that they name: `neighbor_ids`: blocks lie row by row on a map 4 blocks wide. Row b lists in its first neighbor_count[b] entries distinct blocks among b and the up to eight blocks beside it on the map (diagonals included), b first; its other entries equal b. `neighbor_count`: some block has 9.
All inputs are finite; a program needn't handle non-finite values.
Results may differ from the reference program's by a relative error of at most 0.017.
Values may be sent and summed in bfloat16 or wider, within the bound.
A program may use at most 128 MiB of HBM per device.

```python
import math
import jax
import jax.numpy as jnp
from jax import lax

D = 1024
HEADS = 16
FF = 4096
HD = 64
BLK = 128
ROW = 4
MAXN = 9
GRAPHS = 1
LAYERS = 2
TOKENS = 2048
NBLK = 16


def neighbor_table(key):
    blocks = jnp.arange(NBLK, dtype=jnp.int32)
    grid_row = blocks // ROW
    grid_col = blocks % ROW
    step_row = jnp.array([0, -1, -1, -1, 0, 0, 1, 1, 1], dtype=jnp.int32)
    step_col = jnp.array([0, -1, 0, 1, -1, 1, -1, 0, 1], dtype=jnp.int32)
    near_row = grid_row[:, None] + step_row[None, :]
    near_col = grid_col[:, None] + step_col[None, :]
    inside = (near_row >= 0) & (near_row < NBLK // ROW) & (near_col >= 0) & (near_col < ROW)
    keep_link = jax.random.randint(key, (NBLK, 9), 0, 10) < 7
    keep_link = keep_link.at[:, 0].set(True)
    dense_block = (blocks == ROW + 1)[:, None]
    linked = inside & (keep_link | dense_block)
    near_ids = near_row * ROW + near_col
    ordering = jnp.argsort(jnp.where(linked, 0, 1) * 16 + jnp.arange(9, dtype=jnp.int32)[None, :], axis=1)
    sorted_ids = jnp.take_along_axis(near_ids, ordering, axis=1)
    sorted_live = jnp.take_along_axis(linked, ordering, axis=1)
    final_ids = jnp.where(sorted_live, sorted_ids, blocks[:, None])
    counts = jnp.sum(linked.astype(jnp.int32), axis=1)
    return (final_ids.astype(jnp.int32), counts.astype(jnp.int32))


def draw_neighbor_ids(key, part):
    return neighbor_table(jax.random.fold_in(key, 11))[0]


def draw_neighbor_count(key, part):
    return neighbor_table(jax.random.fold_in(key, 11))[1]


def query_base(key):
    return jax.random.normal(jax.random.fold_in(key, 21), (LAYERS, D, D), jnp.float32) / math.sqrt(D)


def draw_w_query(key, part):
    return (1.6 * query_base(key)).astype(jnp.bfloat16)


def draw_w_key(key, part):
    other = jax.random.normal(jax.random.fold_in(key, 22), (LAYERS, D, D), jnp.float32) / math.sqrt(D)
    mixture = 1.6 * other
    return mixture.astype(jnp.bfloat16)


def draw_norm_gain(key, part):
    values = jax.random.uniform(jax.random.fold_in(key, 31), (LAYERS, D), jnp.float32, 0.5, 1.5)
    return values


def draw_tokens(key, part):
    values = jax.random.normal(jax.random.fold_in(key, 41), (GRAPHS, TOKENS, D), jnp.float32)
    return jnp.clip(values, -24.0, 24.0).astype(jnp.bfloat16)


def block_scale(key, extent, shards, smallest, top_value):
    def one(dim, shards_of):
        draws = jax.random.uniform(jax.random.fold_in(jax.random.fold_in(key, 6), dim), (shards_of,), jnp.float32, smallest / len(shards), top_value / len(shards))
        return jnp.repeat(jnp.exp(draws), extent[dim] // shards_of).reshape((-1,) + (1,) * (len(extent) - dim - 1))

    loudness = one(*shards[0])
    for cut in shards[1:]:
        loudness = loudness * one(*cut)
    return loudness


def centred(key, shape, spread, reach, split=(), held_as=jnp.bfloat16):
    result = spread * jax.random.normal(key, shape, jnp.float32)
    if split:
        result = result * block_scale(key, shape, split, -0.22, 0.18)
    return jnp.clip(result, -reach, reach).astype(held_as)


def setup_inputs(seed: int = 0) -> dict:
    key_list = jax.random.split(jax.random.key(seed), 12)
    tokens = draw_tokens(jax.random.fold_in(key_list[11], 71), 0)
    neighbor_ids = draw_neighbor_ids(jax.random.fold_in(key_list[11], 71), 0)
    neighbor_count = draw_neighbor_count(jax.random.fold_in(key_list[11], 71), 0)
    w_query = draw_w_query(jax.random.fold_in(key_list[11], 71), 0)
    w_key = draw_w_key(jax.random.fold_in(key_list[11], 71), 0)
    w_value = centred(key_list[5], (LAYERS, D, D), D ** -0.5, 0.1875, ((0, 2),))
    w_out = centred(key_list[6], (LAYERS, D, D), D ** -0.5, 0.1875, ((0, 2),))
    norm_gain = draw_norm_gain(jax.random.fold_in(key_list[11], 71), 0)
    w_up = centred(key_list[8], (LAYERS, FF, D), D ** -0.5, 0.1875, ((0, 2), (1, 16)))
    w_down = centred(key_list[9], (LAYERS, FF, D), FF ** -0.5, 0.09375, ((0, 2), (1, 16)))
    mlp_gain = jnp.clip(jnp.exp(math.log(2.0) - 1.3862944 * jax.random.uniform(key_list[10], (LAYERS, D), jnp.float32) ** block_scale(key_list[10], (LAYERS, D), ((0, 2),), -0.2, 0.2)), 0.5, 2.0)
    return dict(tokens=tokens, neighbor_ids=neighbor_ids, neighbor_count=neighbor_count, w_query=w_query, w_key=w_key, w_value=w_value, w_out=w_out, norm_gain=norm_gain, w_up=w_up, w_down=w_down, mlp_gain=mlp_gain)


def rms_normed(widened, gain):
    return (widened * lax.rsqrt(lax.optimization_barrier(jnp.mean(widened * widened, axis=-1, keepdims=True)) + 1e-05) * gain).astype(jnp.bfloat16)

def one_layer(inputs, neighbor_ids, neighbor_count, query_weight, key_weight, value_weight, out_weight, gain, up_weight, down_weight, second_gain):
    widened = inputs.astype(jnp.float32)
    normed = rms_normed(widened, gain)
    queries = jnp.dot(normed, query_weight, preferred_element_type=jnp.float32).astype(jnp.bfloat16)
    keys = jnp.dot(normed, key_weight, preferred_element_type=jnp.float32).astype(jnp.bfloat16)
    values = jnp.dot(normed, value_weight, preferred_element_type=jnp.float32).astype(jnp.bfloat16)
    key_blocks = keys.reshape(NBLK, BLK, D)
    value_blocks = values.reshape(NBLK, BLK, D)
    score_scale = 1.0 / math.sqrt(HD)

    def one_block(block):
        query_rows = lax.dynamic_slice_in_dim(queries, block * BLK, BLK, 0).reshape(BLK, HEADS, HD).astype(jnp.float32)
        listed = neighbor_ids[block]
        key_rows = jnp.take(key_blocks, listed, axis=0).reshape(MAXN * BLK, HEADS, HD).astype(jnp.float32)
        value_rows = jnp.take(value_blocks, listed, axis=0).reshape(MAXN * BLK, HEADS, HD).astype(jnp.float32)
        live = jnp.repeat(jnp.arange(MAXN, dtype=jnp.int32) < neighbor_count[block], BLK)
        scores = jnp.einsum('qhd,khd->hqk', query_rows, key_rows) * score_scale
        scores = jnp.where(live[None, None, :], scores, -jnp.inf)
        row_max = lax.optimization_barrier(jnp.max(scores, axis=-1, keepdims=True))
        exponent = jnp.exp(scores - row_max)
        probs = (exponent / lax.optimization_barrier(jnp.sum(exponent, axis=-1, keepdims=True))).astype(jnp.bfloat16)
        mixed = jnp.einsum('hqk,khd->qhd', probs.astype(jnp.float32), value_rows).astype(jnp.bfloat16)
        return mixed.reshape(BLK, D)
    mixed = lax.map(one_block, jnp.arange(NBLK, dtype=jnp.int32)).reshape(NBLK * BLK, D)
    attended = (widened + jnp.dot(mixed, out_weight, preferred_element_type=jnp.float32)).astype(jnp.bfloat16)
    attended_wide = attended.astype(jnp.float32)
    second = rms_normed(attended_wide, second_gain)
    upper_rows = lax.dot_general(second, up_weight, (((1,), (1,)), ((), ())), preferred_element_type=jnp.float32)
    hidden = jax.nn.gelu(upper_rows, approximate=True).astype(jnp.bfloat16)
    return (attended_wide + jnp.dot(hidden, down_weight, preferred_element_type=jnp.float32)).astype(jnp.bfloat16)

def reference(tokens, neighbor_ids, neighbor_count, w_query, w_key, w_value, w_out, norm_gain, w_up, w_down, mlp_gain):
    per_layer = []
    for layer_index in range(LAYERS):
        per_layer.append([])
    for graph_index in range(GRAPHS):
        hidden_state = tokens[graph_index]
        for layer_index in range(LAYERS):
            hidden_state = one_layer(hidden_state, neighbor_ids, neighbor_count, w_query[layer_index], w_key[layer_index], w_value[layer_index], w_out[layer_index], norm_gain[layer_index], w_up[layer_index], w_down[layer_index], mlp_gain[layer_index])
            per_layer[layer_index].append(hidden_state)
    return jnp.stack([jnp.stack(items, axis=0) for items in per_layer], axis=0)
```

```python
import functools
import math

import jax
import jax.numpy as jnp
from jax import lax
from jax.experimental import pallas as pl
from jax.experimental.pallas import tpu as pltpu
from jax.sharding import PartitionSpec as P

HEADS = 16
BLK = 128
ROW = 4
GROUP = 4
HALF = BLK // 2
ORDER = (4, 3, 5, 1, 7, 0, 2, 6, 8)
MESH = pl.DeviceIdType.MESH
NT = (((1,), (1,)), ((), ()))


def normalise(widened, gain):
    mean = jnp.mean(widened * widened, axis=-1, keepdims=True)
    return (widened * lax.rsqrt(mean + 1e-05) * gain).astype(jnp.bfloat16)


def kernel(
    n, ids, count, tokens, w_query, w_key, w_value, w_out, gain, w_up, w_down, second_gain,
    out,
    around, normed, queries, keys, values, mixed, attended, second, hidden, total, leaving,
    landing, finished, wq, wk, wv, wo, up, down, pass_up, pass_down,
    local_sem, x_send, x_recv, o_send, w_send, w_recv, s_send, s_recv, p_send, p_recv, go, f_send,
    r_send, r_recv,
):
    section, seq = lax.axis_index("section"), lax.axis_index("seq")
    row, col = lax.div(seq, ROW), lax.rem(seq, ROW)
    rows = n // ROW
    width = wq.shape[0]
    units = w_up.shape[1]
    mine = lax.rem(row, GROUP)
    members = n // GROUP
    member = lax.div(row, GROUP) * ROW + col
    pairs = HEADS // 2
    plane = members == 4

    def local(src, dst, index):
        return pltpu.make_async_copy(src, dst, local_sem.at[index])

    own_up = pl.ds(pl.multiple_of(member * units, units), units)
    locals_ = [
        local(w_query.at[0], wq, 0),
        local(w_key.at[0], wk, 1),
        local(w_value.at[0], wv, 2),
        local(w_out.at[0], wo, 3),
        local(w_up.at[0], up.at[own_up], 4),
        local(w_down.at[0], down.at[own_up], 5),
    ]
    own_tokens = local(tokens.at[0], around.at[4], 6)

    @pl.when(section == 0)
    def _():
        own_tokens.start()

    for copy in locals_:
        copy.start()

    def beside(slot):
        dr, dc = slot // 3 - 1, slot % 3 - 1
        exists = (row + dr >= 0) & (row + dr < rows) & (col + dc >= 0) & (col + dc < ROW)
        return exists, jnp.clip(row + dr, 0, rows - 1) * ROW + jnp.clip(col + dc, 0, ROW - 1)

    def member_device(place):
        return (lax.div(place, ROW) * GROUP + mine) * ROW + lax.rem(place, ROW)

    def group_device(index):
        return (lax.div(row, GROUP) * GROUP + index) * ROW + col

    barrier = pltpu.get_barrier_semaphore()

    def greet(device):
        for side in range(2):
            pl.semaphore_signal(barrier, inc=1, device_id=(side, device), device_id_type=MESH)

    def greet_member(step, carry):
        greet(member_device(lax.rem(member + step, members)))
        return carry

    lax.fori_loop(1, members, greet_member, 0)
    for step in range(1, GROUP):
        greet(group_device(lax.rem(mine + step, GROUP)))
    pl.semaphore_signal(barrier, inc=1, device_id=(1 - section, seq), device_id_type=MESH)
    expected = 2 * (members - 1) + 2 * (GROUP - 1) + 1
    if rows > GROUP:
        for slot in (1, 3, 5, 7):
            @pl.when(beside(slot)[0])
            def _():
                greet(beside(slot)[1])
            expected = expected + 2 * beside(slot)[0].astype(jnp.int32)

    gain_row = gain[...]

    @pl.when(section == 0)
    def _():
        own_tokens.wait()

    pl.semaphore_wait(barrier, expected)

    def half(slot, h):
        return around.at[slot, pl.ds(HALF * h, HALF)]

    def token_copy(slot, h):
        device = beside(slot)[1]
        return pltpu.make_async_remote_copy(
            half(4, h), half(8 - slot, h), x_send.at[slot, h], x_recv.at[8 - slot, h],
            device_id=(section, device), device_id_type=MESH)

    def result_copy(slot, h):
        device = beside(slot)[1]
        return pltpu.make_async_remote_copy(
            finished.at[pl.ds(HALF * h, HALF)], half(8 - slot, h), o_send.at[slot, h], x_recv.at[8 - slot, h],
            device_id=(1, device), device_id_type=MESH)

    def relay(index, h):
        side, up_or_down = index % 2 * 2, index // 2 * 2
        device = beside(3 * up_or_down + 1)[1]
        slot = 3 * (2 - up_or_down) + side
        exists = beside(3 + side)[0] & beside(3 * up_or_down + 1)[0]
        return exists, pltpu.make_async_remote_copy(
            half(3 + side, h), half(slot, h), f_send.at[index, h], x_recv.at[slot, h],
            device_id=(section, device), device_id_type=MESH)

    def arrival(slot, h):
        return pltpu.make_async_remote_copy(
            finished.at[pl.ds(HALF * h, HALF)], half(slot, h), o_send.at[slot, h], x_recv.at[slot, h],
            device_id=(section, seq), device_id_type=MESH)

    def shard(place):
        return pl.ds(pl.multiple_of(place * units, units), units)

    def weight_copies(step, which):
        device = member_device(lax.rem(member + step, members))
        src, dst = (w_up, up) if which == 0 else (w_down, down)
        return pltpu.make_async_remote_copy(
            src.at[0], dst.at[own_up], w_send.at[2 * step + which], w_recv.at[2 * step + which],
            device_id=(section, device), device_id_type=MESH)

    def weight_arrival(step, which):
        there = shard(lax.rem(member + members - step, members))
        src, dst = (w_up, up) if which == 0 else (w_down, down)
        return pltpu.make_async_remote_copy(
            src.at[0], dst.at[there], w_send.at[2 * step + which], w_recv.at[2 * step + which],
            device_id=(section, seq), device_id_type=MESH)

    def across(bits):
        base = lax.rem(member, 4)
        low, high = lax.rem(base, 2), lax.div(base, 2)
        if bits % 2:
            low = 1 - low
        if bits // 2:
            high = 1 - high
        return 2 * high + low

    def direct(bits, which):
        src, dst = (w_up, up) if which == 0 else (w_down, down)
        return pltpu.make_async_remote_copy(
            src.at[0], dst.at[own_up], w_send.at[2 * bits + which], w_recv.at[2 * bits + which],
            device_id=(section, member_device(across(bits))), device_id_type=MESH)

    def landed(bits, which):
        src, dst = (w_up, up) if which == 0 else (w_down, down)
        return pltpu.make_async_remote_copy(
            src.at[0], dst.at[shard(across(bits))], w_send.at[2 * bits + which], w_recv.at[2 * bits + which],
            device_id=(section, member_device(across(bits))), device_id_type=MESH)

    def onward(which):
        dst = up if which == 0 else down
        there = shard(across(1 + which))
        return pltpu.make_async_remote_copy(
            dst.at[there], dst.at[there], w_send.at[6 + which], w_recv.at[6 + which],
            device_id=(section, member_device(across(2 - which))), device_id_type=MESH)

    def passed(which):
        src, dst = (w_up, pass_up) if which == 0 else (w_down, pass_down)
        return pltpu.make_async_remote_copy(
            src.at[0], dst, r_send.at[which], r_recv.at[which],
            device_id=(1, member_device(across(1 + which))), device_id_type=MESH)

    def passed_on(which, target):
        src, dst = (pass_up, up) if which == 0 else (pass_down, down)
        bits = 1 + which
        device = seq if target == 0 else member_device(across(2 - which))
        index = 2 * bits + which if target == 0 else 6 + which
        return pltpu.make_async_remote_copy(
            src, dst.at[shard(across(bits))], r_send.at[2 + 2 * target + which], w_recv.at[index],
            device_id=(0, device), device_id_type=MESH)

    def each(body):
        if members > 8:
            lax.fori_loop(1, members, body, 0)
        else:
            for step in range(1, members):
                body(step, 0)

    @pl.when(section == 0)
    def _():
        for slot in (3, 5, 1, 7):
            @pl.when(beside(slot)[0])
            def _():
                for h in range(2):
                    token_copy(slot, h).start()

    if plane:
        @pl.when(section == 0)
        def _():
            passed(0).start()
            passed(1).start()
            direct(1, 1).start()
            direct(2, 0).start()

        @pl.when(section == 1)
        def _():
            for which in range(2):
                passed(which).wait_recv()
                for target in (1, 0):
                    passed_on(which, target).start()
            for which in range(2):
                for target in (1, 0):
                    passed_on(which, target).wait_send()
            direct(1, 0).start()
            direct(2, 1).start()
            direct(1, 1).start()
            direct(2, 0).start()
            for which in range(2):
                landed(1 + which, which).wait_recv()
                onward(which).start()
    else:
        @pl.when(section == 1)
        def _():
            pl.semaphore_wait(go, 1)

        def send_weights(step, carry):
            weight_copies(step, 0).start()
            weight_copies(step, 1).start()
            return carry

        each(send_weights)

    def await_half(slot, h):
        exists = beside(slot)[0]

        @pl.when(exists)
        def _():
            arrival(slot, h).wait_recv()

        @pl.when(jnp.logical_not(exists))
        def _():
            around[slot, HALF * h:HALF * h + HALF] = jnp.zeros((HALF, width), jnp.bfloat16)

    @pl.when(section == 1)
    def _():
        for h in range(2):
            arrival(4, h).wait_recv()

    entries = ids[...]
    listed = lax.broadcasted_iota(jnp.int32, entries.shape, 1) < count[...]
    flags = []
    for slot in ORDER:
        exists, device = beside(slot)
        wanted = jnp.where(exists, device, jnp.int32(-1))
        hit = jnp.where(listed & (entries == wanted), 1.0, 0.0)
        flags.append(jnp.broadcast_to(jnp.max(hit, axis=1, keepdims=True), (1, BLK)))
    live_row = jnp.concatenate(flags, axis=1)

    normed[pl.ds(0, BLK)] = normalise(around[4].astype(jnp.float32), gain_row)
    locals_[0].wait()

    score_scale = 1.0 / math.sqrt(width // HEADS)
    product = jnp.dot(normed[pl.ds(0, BLK)], wq[...], preferred_element_type=jnp.float32)
    queries[...] = (product.astype(jnp.bfloat16).astype(jnp.float32) * score_scale).astype(jnp.bfloat16)
    locals_[1].wait()
    locals_[2].wait()

    def project(start, count):
        here, there = pl.ds(0, count * BLK), pl.ds(start * BLK, count * BLK)
        keys[there] = jnp.dot(normed[here], wk[...], preferred_element_type=jnp.float32).astype(jnp.bfloat16)
        values[there] = jnp.dot(normed[here], wv[...], preferred_element_type=jnp.float32).astype(jnp.bfloat16)

    project(0, 1)
    for h in range(2):
        for side in range(2):
            await_half(3 + 2 * side, h)
            for index in (side, side + 2):
                @pl.when(relay(index, h)[0])
                def _():
                    relay(index, h)[1].start()
    for first in (1, 5):
        for place in range(first, first + 4):
            slot = ORDER[place]
            if slot not in (3, 5):
                for h in range(2):
                    await_half(slot, h)
            normed[pl.ds((place - first) * BLK, BLK)] = normalise(around[slot].astype(jnp.float32), gain_row)
        project(first, 4)

    first_half = lax.broadcasted_iota(jnp.int32, (BLK, 128), 1) < 64
    ones = jnp.ones((9 * BLK, 128), jnp.bfloat16)

    def head_pair(pair, carry):
        at = pl.ds(pl.multiple_of(pair * 128, 128), 128)
        q = queries[:, at]
        zero = jnp.zeros_like(q)
        both = jnp.concatenate([jnp.where(first_half, q, zero), jnp.where(first_half, zero, q)], axis=0)
        scores = lax.dot_general(both, keys[:, at], NT, preferred_element_type=jnp.float32)
        scores = jnp.where(live_row > 0.0, scores, -jnp.inf)
        exponent = jnp.exp(scores - jnp.max(scores, axis=-1, keepdims=True)).astype(jnp.bfloat16)
        product = jnp.dot(
            exponent, jnp.concatenate([values[:, at], ones], axis=1), preferred_element_type=jnp.float32)
        product = product[:, :128] / product[:, 128:]
        mixed[:, at] = jnp.where(first_half, product[:BLK], product[BLK:]).astype(jnp.bfloat16)
        return carry

    lax.fori_loop(0, pairs, head_pair, 0, unroll=4)
    locals_[3].wait()
    product = jnp.dot(mixed[...], wo[...], preferred_element_type=jnp.float32)
    attended[...] = (around[4].astype(jnp.float32) + product).astype(jnp.bfloat16)
    second[mine] = normalise(attended[...].astype(jnp.float32), second_gain[...])

    def peer(step):
        if step == 1:
            return mine + 1 - 2 * lax.rem(mine, 2)
        return mine if step == 0 else lax.rem(mine + 2, GROUP) if step == 2 else GROUP - 1 - mine

    def peer_device(step):
        return group_device(peer(step))

    def second_copy(step):
        return pltpu.make_async_remote_copy(
            second.at[mine], second.at[mine], s_send.at[step], s_recv.at[step],
            device_id=(section, peer_device(step)), device_id_type=MESH)

    def second_arrival(step):
        return pltpu.make_async_remote_copy(
            second.at[mine], second.at[peer(step)], s_send.at[step], s_recv.at[step],
            device_id=(section, peer_device(step)), device_id_type=MESH)

    def partial_copy(step):
        return pltpu.make_async_remote_copy(
            leaving.at[step], landing.at[step], p_send.at[step], p_recv.at[step],
            device_id=(section, peer_device(step)), device_id_type=MESH)

    for step in range(1, GROUP):
        second_copy(step).start()

    locals_[4].wait()
    locals_[5].wait()

    if plane:
        for bits in (1, 2, 3):
            for which in range(2):
                @pl.when((section == 0) | (bits != 1 + which))
                def _():
                    landed(bits, which).wait_recv()
    else:
        def await_weights(step, carry):
            weight_arrival(step, 0).wait_recv()
            weight_arrival(step, 1).wait_recv()
            return carry

        each(await_weights)

        @pl.when(section == 0)
        def _():
            pl.semaphore_signal(go, inc=1, device_id=(1, seq), device_id_type=MESH)

    for step in range(GROUP):
        if step:
            second_arrival(step).wait_recv()
        raised = lax.dot_general(second[peer(step)], up[...], NT, preferred_element_type=jnp.float32)
        hidden[...] = jax.nn.gelu(raised, approximate=True).astype(jnp.bfloat16)
        product = jnp.dot(hidden[...], down[...], preferred_element_type=jnp.float32)
        if step:
            leaving[step] = product.astype(jnp.bfloat16)
            partial_copy(step).start()
        else:
            total[...] = product

    gathered = attended[...].astype(jnp.float32) + total[...]
    for step in range(1, GROUP):
        partial_copy(step).wait_recv()
        gathered = gathered + landing[step].astype(jnp.float32)
    result = gathered.astype(jnp.bfloat16)
    finished[...] = result
    out[0, 0] = result

    @pl.when(section == 0)
    def _():
        for slot in (4, 3, 5, 1, 7):
            @pl.when(beside(slot)[0])
            def _():
                for h in range(2):
                    result_copy(slot, h).start()
        for slot in (4, 3, 5, 1, 7):
            @pl.when(beside(slot)[0])
            def _():
                for h in range(2):
                    result_copy(slot, h).wait_send()
                    if slot != 4:
                        token_copy(slot, h).wait_send()

    for index in range(4):
        @pl.when(relay(index, 0)[0])
        def _():
            for h in range(2):
                relay(index, h)[1].wait_send()

    for step in range(1, GROUP):
        second_copy(step).wait_send()
        partial_copy(step).wait_send()

    if plane:
        direct(1, 1).wait_send()
        direct(2, 0).wait_send()

        @pl.when(section == 0)
        def _():
            passed(0).wait_send()
            passed(1).wait_send()

        @pl.when(section == 1)
        def _():
            for which in range(2):
                direct(1 + which, which).wait_send()
                onward(which).wait_send()
    else:
        def drain(step, carry):
            weight_copies(step, 0).wait_send()
            weight_copies(step, 1).wait_send()
            return carry

        each(drain)


def solution(mesh):
    n = mesh.shape["seq"]

    def local(tokens, ids, count, w_query, w_key, w_value, w_out, gain, w_up, w_down, second_gain):
        width = tokens.shape[-1]
        held = w_up.shape[1] * n // GROUP
        members = n // GROUP
        bf16, f32 = jnp.bfloat16, jnp.float32
        any_ = pl.BlockSpec(memory_space=pltpu.HBM)
        vmem = pl.BlockSpec(memory_space=pltpu.VMEM)
        dma = pltpu.SemaphoreType.DMA
        return pl.pallas_call(
            functools.partial(kernel, n),
            out_shape=jax.ShapeDtypeStruct((1,) + tokens.shape, bf16),
            in_specs=[vmem, vmem, any_, any_, any_, any_, any_, vmem, any_, any_, vmem],
            out_specs=vmem,
            scratch_shapes=[
                pltpu.VMEM((9, BLK, width), bf16),
                pltpu.VMEM((4 * BLK, width), bf16),
                pltpu.VMEM((BLK, width), bf16),
                pltpu.VMEM((9 * BLK, width), bf16),
                pltpu.VMEM((9 * BLK, width), bf16),
                pltpu.VMEM((BLK, width), bf16),
                pltpu.VMEM((BLK, width), bf16),
                pltpu.VMEM((GROUP, BLK, width), bf16),
                pltpu.VMEM((BLK, held), bf16),
                pltpu.VMEM((BLK, width), f32),
                pltpu.VMEM((GROUP, BLK, width), bf16),
                pltpu.VMEM((GROUP, BLK, width), bf16),
                pltpu.VMEM((BLK, width), bf16),
                pltpu.VMEM((width, width), bf16),
                pltpu.VMEM((width, width), bf16),
                pltpu.VMEM((width, width), bf16),
                pltpu.VMEM((width, width), bf16),
                pltpu.VMEM((held, width), bf16),
                pltpu.VMEM((held, width), bf16),
                pltpu.VMEM((w_up.shape[1], width), bf16),
                pltpu.VMEM((w_up.shape[1], width), bf16),
                dma((7,)),
                dma((9, 2)),
                dma((9, 2)),
                dma((9, 2)),
                dma((2 * members,)),
                dma((2 * members,)),
                dma((GROUP,)),
                dma((GROUP,)),
                dma((GROUP,)),
                dma((GROUP,)),
                pltpu.SemaphoreType.REGULAR,
                dma((4, 2)),
                dma((6,)),
                dma((2,)),
            ],
            compiler_params=pltpu.CompilerParams(
                collective_id=0, has_side_effects=True, vmem_limit_bytes=56 * 1024 * 1024),
        )(ids, count.reshape(1, 1), tokens, w_query, w_key, w_value, w_out, gain, w_up, w_down, second_gain)

    in_specs = (
        P(None, "seq", None),
        P("seq", None),
        P("seq"),
        P("section", None, None),
        P("section", None, None),
        P("section", None, None),
        P("section", None, None),
        P("section", None),
        P("section", "seq", None),
        P("section", "seq", None),
        P("section", None),
    )
    return jax.shard_map(
        local, mesh=mesh, in_specs=in_specs, out_specs=P("section", None, "seq", None), check_vma=False)
```

```python
import functools
import math

import jax
import jax.numpy as jnp
from jax import lax
from jax.experimental import pallas as pl
from jax.experimental.pallas import tpu as pltpu
from jax.sharding import PartitionSpec as P

HEADS = 16
BLK = 128
ROW = 4
GROUP = 4
HALF = BLK // 2
ORDER = (4, 3, 5, 1, 7, 0, 2, 6, 8)
MESH = pl.DeviceIdType.MESH
NT = (((1,), (1,)), ((), ()))


def normalise(widened, gain):
    mean = jnp.mean(widened * widened, axis=-1, keepdims=True)
    return (widened * lax.rsqrt(mean + 1e-05) * gain).astype(jnp.bfloat16)


def kernel(
    n, ids, count, tokens, w_query, w_key, w_value, w_out, gain, w_up, w_down, second_gain,
    out,
    around, normed, queries, keys, values, mixed, attended, second, hidden, total, leaving,
    landing, finished, wq, wk, wv, wo, up, down, pass_up, pass_down, near_sum, near_top, hop,
    local_sem, x_send, x_recv, o_send, w_send, w_recv, s_send, s_recv, p_send, p_recv, go, f_send,
    r_send, r_recv, h_send, h_recv,
):
    section, seq = lax.axis_index("section"), lax.axis_index("seq")
    row, col = lax.div(seq, ROW), lax.rem(seq, ROW)
    rows = n // ROW
    width = wq.shape[0]
    units = w_up.shape[1]
    mine = lax.rem(row, GROUP)
    members = n // GROUP
    member = lax.div(row, GROUP) * ROW + col
    pairs = HEADS // 2
    plane = members == 4

    def local(src, dst, index):
        return pltpu.make_async_copy(src, dst, local_sem.at[index])

    own_up = pl.ds(pl.multiple_of(member * units, units), units)
    locals_ = [
        local(w_query.at[0], wq, 0),
        local(w_key.at[0], wk, 1),
        local(w_value.at[0], wv, 2),
        local(w_out.at[0], wo, 3),
        local(w_up.at[0], up.at[own_up], 4),
        local(w_down.at[0], down.at[own_up], 5),
    ]
    own_tokens = local(tokens.at[0], around.at[4], 6)

    @pl.when(section == 0)
    def _():
        own_tokens.start()

    for copy in locals_:
        copy.start()

    def beside(slot):
        dr, dc = slot // 3 - 1, slot % 3 - 1
        exists = (row + dr >= 0) & (row + dr < rows) & (col + dc >= 0) & (col + dc < ROW)
        return exists, jnp.clip(row + dr, 0, rows - 1) * ROW + jnp.clip(col + dc, 0, ROW - 1)

    def member_device(place):
        return (lax.div(place, ROW) * GROUP + mine) * ROW + lax.rem(place, ROW)

    def group_device(index):
        return (lax.div(row, GROUP) * GROUP + index) * ROW + col

    barrier = pltpu.get_barrier_semaphore()

    def greet(device):
        for side in range(2):
            pl.semaphore_signal(barrier, inc=1, device_id=(side, device), device_id_type=MESH)

    def greet_member(step, carry):
        greet(member_device(lax.rem(member + step, members)))
        return carry

    lax.fori_loop(1, members, greet_member, 0)
    for step in range(1, GROUP):
        greet(group_device(lax.rem(mine + step, GROUP)))
    pl.semaphore_signal(barrier, inc=1, device_id=(1 - section, seq), device_id_type=MESH)
    expected = 2 * (members - 1) + 2 * (GROUP - 1) + 1
    if rows > GROUP:
        for slot in (1, 3, 5, 7):
            @pl.when(beside(slot)[0])
            def _():
                greet(beside(slot)[1])
            expected = expected + 2 * beside(slot)[0].astype(jnp.int32)

    gain_row = gain[...]

    @pl.when(section == 0)
    def _():
        own_tokens.wait()

    pl.semaphore_wait(barrier, expected)

    def half(slot, h):
        return around.at[slot, pl.ds(HALF * h, HALF)]

    def token_copy(slot, h):
        device = beside(slot)[1]
        return pltpu.make_async_remote_copy(
            half(4, h), half(8 - slot, h), x_send.at[slot, h], x_recv.at[8 - slot, h],
            device_id=(section, device), device_id_type=MESH)

    def result_copy(slot, h):
        device = beside(slot)[1]
        return pltpu.make_async_remote_copy(
            finished.at[pl.ds(HALF * h, HALF)], half(8 - slot, h), o_send.at[slot, h], x_recv.at[8 - slot, h],
            device_id=(1, device), device_id_type=MESH)

    def relay(index, h):
        side, up_or_down = index % 2 * 2, index // 2 * 2
        device = beside(3 * up_or_down + 1)[1]
        slot = 3 * (2 - up_or_down) + side
        exists = beside(3 + side)[0] & beside(3 * up_or_down + 1)[0]
        return exists, pltpu.make_async_remote_copy(
            half(3 + side, h), half(slot, h), f_send.at[index, h], x_recv.at[slot, h],
            device_id=(section, device), device_id_type=MESH)

    def arrival(slot, h):
        return pltpu.make_async_remote_copy(
            finished.at[pl.ds(HALF * h, HALF)], half(slot, h), o_send.at[slot, h], x_recv.at[slot, h],
            device_id=(section, seq), device_id_type=MESH)

    def spread(copy, h):
        right = col < ROW // 2
        for slot, when in ((5, right), (3, col >= ROW // 2), (1, True), (7, True), (3, right), (5, col >= ROW // 2)):
            @pl.when(when & beside(slot)[0])
            def _():
                copy(slot, h).start()

    def shard(place):
        return pl.ds(pl.multiple_of(place * units, units), units)

    def weight_copies(step, which):
        device = member_device(lax.rem(member + step, members))
        src, dst = (w_up, up) if which == 0 else (w_down, down)
        return pltpu.make_async_remote_copy(
            src.at[0], dst.at[own_up], w_send.at[2 * step + which], w_recv.at[2 * step + which],
            device_id=(section, device), device_id_type=MESH)

    def weight_arrival(step, which):
        there = shard(lax.rem(member + members - step, members))
        src, dst = (w_up, up) if which == 0 else (w_down, down)
        return pltpu.make_async_remote_copy(
            src.at[0], dst.at[there], w_send.at[2 * step + which], w_recv.at[2 * step + which],
            device_id=(section, seq), device_id_type=MESH)

    def across(bits):
        base = lax.rem(member, 4)
        low, high = lax.rem(base, 2), lax.div(base, 2)
        if bits % 2:
            low = 1 - low
        if bits // 2:
            high = 1 - high
        return 2 * high + low

    def direct(bits, which):
        src, dst = (w_up, up) if which == 0 else (w_down, down)
        return pltpu.make_async_remote_copy(
            src.at[0], dst.at[own_up], w_send.at[2 * bits + which], w_recv.at[2 * bits + which],
            device_id=(section, member_device(across(bits))), device_id_type=MESH)

    def landed(bits, which):
        src, dst = (w_up, up) if which == 0 else (w_down, down)
        return pltpu.make_async_remote_copy(
            src.at[0], dst.at[shard(across(bits))], w_send.at[2 * bits + which], w_recv.at[2 * bits + which],
            device_id=(section, member_device(across(bits))), device_id_type=MESH)

    def onward(which):
        dst = up if which == 0 else down
        there = shard(across(1 + which))
        return pltpu.make_async_remote_copy(
            dst.at[there], dst.at[there], w_send.at[6 + which], w_recv.at[6 + which],
            device_id=(section, member_device(across(2 - which))), device_id_type=MESH)

    def passed(which):
        src, dst = (w_up, pass_up) if which == 0 else (w_down, pass_down)
        return pltpu.make_async_remote_copy(
            src.at[0], dst, r_send.at[which], r_recv.at[which],
            device_id=(1, member_device(across(1 + which))), device_id_type=MESH)

    def passed_on(which, target):
        src, dst = (pass_up, up) if which == 0 else (pass_down, down)
        bits = 1 + which
        device = seq if target == 0 else member_device(across(2 - which))
        index = 2 * bits + which if target == 0 else 6 + which
        return pltpu.make_async_remote_copy(
            src, dst.at[shard(across(bits))], r_send.at[2 + 2 * target + which], w_recv.at[index],
            device_id=(0, device), device_id_type=MESH)

    def each(body):
        if members > 8:
            lax.fori_loop(1, members, body, 0)
        else:
            for step in range(1, members):
                body(step, 0)

    @pl.when(section == 0)
    def _():
        for h in range(2):
            spread(token_copy, h)

    low = mine < 2
    middle = (mine == 1) | (mine == 2)

    def peer(step):
        if step < 2:
            return mine if step == 0 else mine + 1 - 2 * lax.rem(mine, 2)
        return jnp.where(low, step, 3 - step)

    def rows_of(h):
        return pl.ds(HALF * h, HALF)

    def second_copy(h):
        return pltpu.make_async_remote_copy(
            second.at[mine, rows_of(h)], second.at[mine, rows_of(h)], s_send.at[0, h], s_recv.at[1, h],
            device_id=(section, group_device(peer(1))), device_id_type=MESH)

    def hop_copy(h):
        place = jnp.where(middle, 0, 1)
        return pltpu.make_async_remote_copy(
            second.at[mine, rows_of(h)], hop.at[place, rows_of(h)], s_send.at[1, h], h_recv.at[place, h],
            device_id=(1 - section, group_device(jnp.where(low, 2, 1))), device_id_type=MESH)

    def hop_arrival(place, h):
        return pltpu.make_async_remote_copy(
            second.at[mine, rows_of(h)], hop.at[place, rows_of(h)], s_send.at[1, h], h_recv.at[place, h],
            device_id=(1 - section, group_device(peer(2 + place))), device_id_type=MESH)

    def hop_on(place, h, target):
        device = seq if target == 0 else group_device(peer(1))
        return pltpu.make_async_remote_copy(
            hop.at[place, rows_of(h)], second.at[peer(2 + place), rows_of(h)],
            h_send.at[place, h, target], s_recv.at[2 + place, h],
            device_id=(1 - section, device), device_id_type=MESH)

    def pass_second():
        @pl.when(middle)
        def _():
            for place in range(2):
                for h in range(2):
                    hop_arrival(place, h).wait_recv()
                    hop_on(place, h, 1).start()
                    hop_on(place, h, 0).start()

    def second_arrival(step, h):
        return pltpu.make_async_remote_copy(
            second.at[mine, rows_of(h)], second.at[peer(step), rows_of(h)], s_send.at[0, h], s_recv.at[step, h],
            device_id=(section, group_device(peer(step))), device_id_type=MESH)

    def partial_copy(step, h):
        place = 1 if step == 1 else 2 + lax.rem(mine, 2)
        return pltpu.make_async_remote_copy(
            leaving.at[step, rows_of(h)], landing.at[place, rows_of(h)], p_send.at[step, h], p_recv.at[place, h],
            device_id=(section, group_device(peer(step))), device_id_type=MESH)

    def partial_arrival(place, h):
        return pltpu.make_async_remote_copy(
            leaving.at[place, rows_of(h)], landing.at[place, rows_of(h)], p_send.at[place, h], p_recv.at[place, h],
            device_id=(section, group_device(peer(1))), device_id_type=MESH)

    if plane:
        @pl.when(section == 0)
        def _():
            passed(0).start()
            passed(1).start()
            direct(1, 1).start()
            direct(2, 0).start()

        @pl.when(section == 1)
        def _():
            for which in range(2):
                passed(which).wait_recv()
                for target in (1, 0):
                    passed_on(which, target).start()
            for which in range(2):
                for target in (1, 0):
                    passed_on(which, target).wait_send()
            direct(1, 0).start()
            direct(2, 1).start()
            direct(1, 1).start()
            direct(2, 0).start()
            pass_second()
            for which in range(2):
                landed(1 + which, which).wait_recv()
                onward(which).start()
    else:
        @pl.when(section == 1)
        def _():
            pass_second()
            pl.semaphore_wait(go, 1)

        def send_weights(step, carry):
            weight_copies(step, 0).start()
            weight_copies(step, 1).start()
            return carry

        each(send_weights)

    def await_half(slot, h):
        exists = beside(slot)[0]

        @pl.when(exists)
        def _():
            arrival(slot, h).wait_recv()

        @pl.when(jnp.logical_not(exists))
        def _():
            around[slot, HALF * h:HALF * h + HALF] = jnp.zeros((HALF, width), jnp.bfloat16)

    @pl.when(section == 1)
    def _():
        for h in range(2):
            arrival(4, h).wait_recv()

    entries = ids[...]
    listed = lax.broadcasted_iota(jnp.int32, entries.shape, 1) < count[...]
    flags = []
    for slot in ORDER:
        exists, device = beside(slot)
        wanted = jnp.where(exists, device, jnp.int32(-1))
        hit = jnp.where(listed & (entries == wanted), 1.0, 0.0)
        flags.append(jnp.broadcast_to(jnp.max(hit, axis=1, keepdims=True), (1, BLK)))
    live_row = jnp.concatenate(flags, axis=1)

    normed[pl.ds(0, BLK)] = normalise(around[4].astype(jnp.float32), gain_row)
    locals_[0].wait()

    score_scale = 1.0 / math.sqrt(width // HEADS)
    product = jnp.dot(normed[pl.ds(0, BLK)], wq[...], preferred_element_type=jnp.float32)
    queries[...] = (product.astype(jnp.bfloat16).astype(jnp.float32) * score_scale).astype(jnp.bfloat16)
    locals_[1].wait()
    locals_[2].wait()

    def project(start, count):
        here, there = pl.ds(0, count * BLK), pl.ds(start * BLK, count * BLK)
        keys[there] = jnp.dot(normed[here], wk[...], preferred_element_type=jnp.float32).astype(jnp.bfloat16)
        values[there] = jnp.dot(normed[here], wv[...], preferred_element_type=jnp.float32).astype(jnp.bfloat16)

    project(0, 1)
    for h in range(2):
        for side in range(2):
            await_half(3 + 2 * side, h)
            for index in (side, side + 2):
                @pl.when(relay(index, h)[0])
                def _():
                    relay(index, h)[1].start()
    def gather(first):
        for place in range(first, first + 4):
            slot = ORDER[place]
            if slot not in (3, 5):
                for h in range(2):
                    await_half(slot, h)
            normed[pl.ds((place - first) * BLK, BLK)] = normalise(around[slot].astype(jnp.float32), gain_row)
        project(first, 4)

    first_half = lax.broadcasted_iota(jnp.int32, (BLK, 128), 1) < 64

    def score(at, there):
        q = queries[:, at]
        zero = jnp.zeros_like(q)
        both = jnp.concatenate([jnp.where(first_half, q, zero), jnp.where(first_half, zero, q)], axis=0)
        scores = lax.dot_general(both, keys[there, at], NT, preferred_element_type=jnp.float32)
        return jnp.where(live_row[:, there] > 0.0, scores, -jnp.inf)

    def weigh(scores, top, at, there):
        ones = jnp.ones((scores.shape[1], 128), jnp.bfloat16)
        return jnp.dot(
            jnp.exp(scores - top).astype(jnp.bfloat16), jnp.concatenate([values[there, at], ones], axis=1),
            preferred_element_type=jnp.float32)

    near, far = slice(0, 5 * BLK), slice(5 * BLK, 9 * BLK)

    def near_pair(pair, carry):
        at = pl.ds(pl.multiple_of(pair * 128, 128), 128)
        scores = score(at, near)
        top = jnp.max(scores, axis=-1, keepdims=True)
        near_sum[pair] = weigh(scores, top, at, near)
        near_top[pair] = jnp.broadcast_to(top, (2 * BLK, 128))
        return carry

    def far_pair(pair, carry):
        at = pl.ds(pl.multiple_of(pair * 128, 128), 128)
        scores = score(at, far)
        before = near_top[pair]
        top = jnp.maximum(before, jnp.max(scores, axis=-1, keepdims=True))
        kept = jnp.exp(before - top)
        product = near_sum[pair] * jnp.concatenate([kept, kept], axis=1) + weigh(scores, top[:, :1], at, far)
        product = product[:, :128] / product[:, 128:]
        mixed[:, at] = jnp.where(first_half, product[:BLK], product[BLK:]).astype(jnp.bfloat16)
        return carry

    gather(1)
    lax.fori_loop(0, pairs, near_pair, 0, unroll=4)
    gather(5)
    lax.fori_loop(0, pairs, far_pair, 0, unroll=4)
    locals_[3].wait()
    product = jnp.dot(mixed[...], wo[...], preferred_element_type=jnp.float32)
    attended[...] = (around[4].astype(jnp.float32) + product).astype(jnp.bfloat16)
    second[mine] = normalise(attended[...].astype(jnp.float32), second_gain[...])

    for h in range(2):
        hop_copy(h).start()
    for h in range(2):
        second_copy(h).start()

    locals_[4].wait()
    locals_[5].wait()

    if plane:
        for bits in (1, 2, 3):
            for which in range(2):
                @pl.when((section == 0) | (bits != 1 + which))
                def _():
                    landed(bits, which).wait_recv()
    else:
        def await_weights(step, carry):
            weight_arrival(step, 0).wait_recv()
            weight_arrival(step, 1).wait_recv()
            return carry

        each(await_weights)

        @pl.when(section == 0)
        def _():
            pl.semaphore_signal(go, inc=1, device_id=(1, seq), device_id_type=MESH)

    for step in range(GROUP):
        if step:
            for h in range(2):
                second_arrival(step, h).wait_recv()
        raised = lax.dot_general(second[peer(step)], up[...], NT, preferred_element_type=jnp.float32)
        hidden[...] = jax.nn.gelu(raised, approximate=True).astype(jnp.bfloat16)
        product = jnp.dot(hidden[...], down[...], preferred_element_type=jnp.float32)
        if step:
            leaving[step] = product.astype(jnp.bfloat16)
            for h in range(2):
                partial_copy(step, h).start()
        else:
            total[...] = product

    for h in range(2):
        at = slice(HALF * h, HALF * h + HALF)
        gathered = attended[at].astype(jnp.float32) + total[at]
        for step in range(1, GROUP):
            partial_arrival(step, h).wait_recv()
            gathered = gathered + landing[step, at].astype(jnp.float32)
        result = gathered.astype(jnp.bfloat16)
        finished[at] = result
        out[0, 0, at] = result

        @pl.when(section == 0)
        def _():
            spread(result_copy, h)
            result_copy(4, h).start()

    @pl.when(section == 0)
    def _():
        for slot in (4, 3, 5, 1, 7):
            @pl.when(beside(slot)[0])
            def _():
                for h in range(2):
                    result_copy(slot, h).wait_send()
                    if slot != 4:
                        token_copy(slot, h).wait_send()

    for index in range(4):
        @pl.when(relay(index, 0)[0])
        def _():
            for h in range(2):
                relay(index, h)[1].wait_send()

    @pl.when(section == 0)
    def _():
        pass_second()

    for h in range(2):
        second_copy(h).wait_send()
        hop_copy(h).wait_send()

    @pl.when(middle)
    def _():
        for place in range(2):
            for h in range(2):
                for target in range(2):
                    hop_on(place, h, target).wait_send()

    for step in range(1, GROUP):
        for h in range(2):
            partial_copy(step, h).wait_send()


    if plane:
        direct(1, 1).wait_send()
        direct(2, 0).wait_send()

        @pl.when(section == 0)
        def _():
            passed(0).wait_send()
            passed(1).wait_send()

        @pl.when(section == 1)
        def _():
            for which in range(2):
                direct(1 + which, which).wait_send()
                onward(which).wait_send()
    else:
        def drain(step, carry):
            weight_copies(step, 0).wait_send()
            weight_copies(step, 1).wait_send()
            return carry

        each(drain)


def solution(mesh):
    n = mesh.shape["seq"]

    def local(tokens, ids, count, w_query, w_key, w_value, w_out, gain, w_up, w_down, second_gain):
        width = tokens.shape[-1]
        held = w_up.shape[1] * n // GROUP
        members = n // GROUP
        bf16, f32 = jnp.bfloat16, jnp.float32
        any_ = pl.BlockSpec(memory_space=pltpu.HBM)
        vmem = pl.BlockSpec(memory_space=pltpu.VMEM)
        dma = pltpu.SemaphoreType.DMA
        return pl.pallas_call(
            functools.partial(kernel, n),
            out_shape=pltpu.VMEM((1,) + tokens.shape, bf16),
            in_specs=[vmem, vmem, any_, any_, any_, any_, any_, vmem, any_, any_, vmem],
            out_specs=vmem,
            scratch_shapes=[
                pltpu.VMEM((9, BLK, width), bf16),
                pltpu.VMEM((4 * BLK, width), bf16),
                pltpu.VMEM((BLK, width), bf16),
                pltpu.VMEM((9 * BLK, width), bf16),
                pltpu.VMEM((9 * BLK, width), bf16),
                pltpu.VMEM((BLK, width), bf16),
                pltpu.VMEM((BLK, width), bf16),
                pltpu.VMEM((GROUP, BLK, width), bf16),
                pltpu.VMEM((BLK, held), bf16),
                pltpu.VMEM((BLK, width), f32),
                pltpu.VMEM((GROUP, BLK, width), bf16),
                pltpu.VMEM((GROUP, BLK, width), bf16),
                pltpu.VMEM((BLK, width), bf16),
                pltpu.VMEM((width, width), bf16),
                pltpu.VMEM((width, width), bf16),
                pltpu.VMEM((width, width), bf16),
                pltpu.VMEM((width, width), bf16),
                pltpu.VMEM((held, width), bf16),
                pltpu.VMEM((held, width), bf16),
                pltpu.VMEM((w_up.shape[1], width), bf16),
                pltpu.VMEM((w_up.shape[1], width), bf16),
                pltpu.VMEM((HEADS // 2, 2 * BLK, 256), f32),
                pltpu.VMEM((HEADS // 2, 2 * BLK, 128), f32),
                pltpu.VMEM((2, BLK, width), bf16),
                dma((7,)),
                dma((9, 2)),
                dma((9, 2)),
                dma((9, 2)),
                dma((2 * members,)),
                dma((2 * members,)),
                dma((2, 2)),
                dma((GROUP, 2)),
                dma((GROUP, 2)),
                dma((GROUP, 2)),
                pltpu.SemaphoreType.REGULAR,
                dma((4, 2)),
                dma((6,)),
                dma((2,)),
                dma((2, 2, 2)),
                dma((2, 2)),
            ],
            compiler_params=pltpu.CompilerParams(
                collective_id=0, has_side_effects=True, vmem_limit_bytes=56 * 1024 * 1024),
        )(ids, count.reshape(1, 1), tokens, w_query, w_key, w_value, w_out, gain, w_up, w_down, second_gain)

    in_specs = (
        P(None, "seq", None),
        P("seq", None),
        P("seq"),
        P("section", None, None),
        P("section", None, None),
        P("section", None, None),
        P("section", None, None),
        P("section", None),
        P("section", "seq", None),
        P("section", "seq", None),
        P("section", None),
    )
    return jax.shard_map(
        local, mesh=mesh, in_specs=in_specs, out_specs=P("section", None, "seq", None), check_vma=False)
```

```python
import functools
import math

import jax
import jax.numpy as jnp
from jax import lax
from jax.experimental import pallas as pl
from jax.experimental.pallas import tpu as pltpu
from jax.sharding import PartitionSpec as P

HEADS = 16
BLK = 128
ROW = 4
GROUP = 4
HALF = BLK // 2
ORDER = (4, 3, 5, 1, 7, 0, 2, 6, 8)
MESH = pl.DeviceIdType.MESH
NT = (((1,), (1,)), ((), ()))


def normalise(widened, gain):
    mean = jnp.mean(widened * widened, axis=-1, keepdims=True)
    return (widened * lax.rsqrt(mean + 1e-05) * gain).astype(jnp.bfloat16)


def kernel(
    n, ids, count, tokens, w_query, w_key, w_value, w_out, gain, w_up, w_down, second_gain,
    out,
    around, normed, queries, keys, values, mixed, attended, second, hidden, total, leaving,
    landing, finished, wq, wk, wv, wo, up, down, pass_up, pass_down, near_sum, near_top, hop,
    local_sem, x_send, x_recv, o_send, w_send, w_recv, s_send, s_recv, p_send, p_recv, go, f_send,
    r_send, r_recv, h_send, h_recv,
):
    section, seq = lax.axis_index("section"), lax.axis_index("seq")
    row, col = lax.div(seq, ROW), lax.rem(seq, ROW)
    rows = n // ROW
    width = wq.shape[0]
    units = w_up.shape[1]
    mine = lax.rem(row, GROUP)
    members = n // GROUP
    member = lax.div(row, GROUP) * ROW + col
    pairs = HEADS // 2
    plane = members == 4

    def local(src, dst, index):
        return pltpu.make_async_copy(src, dst, local_sem.at[index])

    own_up = pl.ds(pl.multiple_of(member * units, units), units)
    locals_ = [
        local(w_query.at[0], wq, 0),
        local(w_key.at[0], wk, 1),
        local(w_value.at[0], wv, 2),
        local(w_out.at[0], wo, 3),
        local(w_up.at[0], up.at[own_up], 4),
        local(w_down.at[0], down.at[own_up], 5),
    ]
    own_tokens = local(tokens.at[0], around.at[4], 6)

    @pl.when(section == 0)
    def _():
        own_tokens.start()

    for copy in locals_:
        copy.start()

    def beside(slot):
        dr, dc = slot // 3 - 1, slot % 3 - 1
        exists = (row + dr >= 0) & (row + dr < rows) & (col + dc >= 0) & (col + dc < ROW)
        return exists, jnp.clip(row + dr, 0, rows - 1) * ROW + jnp.clip(col + dc, 0, ROW - 1)

    def member_device(place):
        return (lax.div(place, ROW) * GROUP + mine) * ROW + lax.rem(place, ROW)

    def group_device(index):
        return (lax.div(row, GROUP) * GROUP + index) * ROW + col

    barrier = pltpu.get_barrier_semaphore()

    def greet(device):
        for side in range(2):
            pl.semaphore_signal(barrier, inc=1, device_id=(side, device), device_id_type=MESH)

    def greet_member(step, carry):
        greet(member_device(lax.rem(member + step, members)))
        return carry

    lax.fori_loop(1, members, greet_member, 0)
    for step in range(1, GROUP):
        greet(group_device(lax.rem(mine + step, GROUP)))
    pl.semaphore_signal(barrier, inc=1, device_id=(1 - section, seq), device_id_type=MESH)
    expected = 2 * (members - 1) + 2 * (GROUP - 1) + 1
    if rows > GROUP:
        for slot in (1, 3, 5, 7):
            @pl.when(beside(slot)[0])
            def _():
                greet(beside(slot)[1])
            expected = expected + 2 * beside(slot)[0].astype(jnp.int32)

    gain_row = gain[...]

    @pl.when(section == 0)
    def _():
        own_tokens.wait()

    pl.semaphore_wait(barrier, expected)

    def half(slot, h):
        return around.at[slot, pl.ds(HALF * h, HALF)]

    def token_copy(slot, h):
        device = beside(slot)[1]
        return pltpu.make_async_remote_copy(
            half(4, h), half(8 - slot, h), x_send.at[slot, h], x_recv.at[8 - slot, h],
            device_id=(section, device), device_id_type=MESH)

    def result_copy(slot, h):
        device = beside(slot)[1]
        return pltpu.make_async_remote_copy(
            finished.at[pl.ds(HALF * h, HALF)], half(8 - slot, h), o_send.at[slot, h], x_recv.at[8 - slot, h],
            device_id=(1, device), device_id_type=MESH)

    def relay(index, h):
        side, up_or_down = index % 2 * 2, index // 2 * 2
        device = beside(3 * up_or_down + 1)[1]
        slot = 3 * (2 - up_or_down) + side
        exists = beside(3 + side)[0] & beside(3 * up_or_down + 1)[0]
        return exists, pltpu.make_async_remote_copy(
            half(3 + side, h), half(slot, h), f_send.at[index, h], x_recv.at[slot, h],
            device_id=(section, device), device_id_type=MESH)

    def arrival(slot, h):
        return pltpu.make_async_remote_copy(
            finished.at[pl.ds(HALF * h, HALF)], half(slot, h), o_send.at[slot, h], x_recv.at[slot, h],
            device_id=(section, seq), device_id_type=MESH)

    def spread(copy, h):
        right = col < ROW // 2
        for slot, when in ((5, right), (3, col >= ROW // 2), (1, True), (7, True), (3, right), (5, col >= ROW // 2)):
            @pl.when(when & beside(slot)[0])
            def _():
                copy(slot, h).start()

    def shard(place):
        return pl.ds(pl.multiple_of(place * units, units), units)

    def weight_copies(step, which):
        device = member_device(lax.rem(member + step, members))
        src, dst = (w_up, up) if which == 0 else (w_down, down)
        return pltpu.make_async_remote_copy(
            src.at[0], dst.at[own_up], w_send.at[2 * step + which], w_recv.at[2 * step + which],
            device_id=(section, device), device_id_type=MESH)

    def weight_arrival(step, which):
        there = shard(lax.rem(member + members - step, members))
        src, dst = (w_up, up) if which == 0 else (w_down, down)
        return pltpu.make_async_remote_copy(
            src.at[0], dst.at[there], w_send.at[2 * step + which], w_recv.at[2 * step + which],
            device_id=(section, seq), device_id_type=MESH)

    def across(bits):
        base = lax.rem(member, 4)
        low, high = lax.rem(base, 2), lax.div(base, 2)
        if bits % 2:
            low = 1 - low
        if bits // 2:
            high = 1 - high
        return 2 * high + low

    def direct(bits, which):
        src, dst = (w_up, up) if which == 0 else (w_down, down)
        return pltpu.make_async_remote_copy(
            src.at[0], dst.at[own_up], w_send.at[2 * bits + which], w_recv.at[2 * bits + which],
            device_id=(section, member_device(across(bits))), device_id_type=MESH)

    def landed(bits, which):
        src, dst = (w_up, up) if which == 0 else (w_down, down)
        return pltpu.make_async_remote_copy(
            src.at[0], dst.at[shard(across(bits))], w_send.at[2 * bits + which], w_recv.at[2 * bits + which],
            device_id=(section, member_device(across(bits))), device_id_type=MESH)

    def onward(which):
        dst = up if which == 0 else down
        there = shard(across(1 + which))
        return pltpu.make_async_remote_copy(
            dst.at[there], dst.at[there], w_send.at[6 + which], w_recv.at[6 + which],
            device_id=(section, member_device(across(2 - which))), device_id_type=MESH)

    def passed(which):
        src, dst = (w_up, pass_up) if which == 0 else (w_down, pass_down)
        return pltpu.make_async_remote_copy(
            src.at[0], dst, r_send.at[which], r_recv.at[which],
            device_id=(1, member_device(across(1 + which))), device_id_type=MESH)

    def passed_on(which, target):
        src, dst = (pass_up, up) if which == 0 else (pass_down, down)
        bits = 1 + which
        device = seq if target == 0 else member_device(across(2 - which))
        index = 2 * bits + which if target == 0 else 6 + which
        return pltpu.make_async_remote_copy(
            src, dst.at[shard(across(bits))], r_send.at[2 + 2 * target + which], w_recv.at[index],
            device_id=(0, device), device_id_type=MESH)

    def each(body):
        if members > 8:
            lax.fori_loop(1, members, body, 0)
        else:
            for step in range(1, members):
                body(step, 0)

    @pl.when(section == 0)
    def _():
        for h in range(2):
            spread(token_copy, h)

    low = mine < 2
    middle = (mine == 1) | (mine == 2)

    def peer(step):
        if step < 2:
            return mine if step == 0 else mine + 1 - 2 * lax.rem(mine, 2)
        return jnp.where(low, step, 3 - step)

    def rows_of(h):
        return pl.ds(HALF * h, HALF)

    def second_copy(h):
        return pltpu.make_async_remote_copy(
            second.at[mine, rows_of(h)], second.at[mine, rows_of(h)], s_send.at[0, h], s_recv.at[1, h],
            device_id=(section, group_device(peer(1))), device_id_type=MESH)

    def hop_copy(h):
        place = jnp.where(middle, 0, 1)
        return pltpu.make_async_remote_copy(
            second.at[mine, rows_of(h)], hop.at[place, rows_of(h)], s_send.at[1, h], h_recv.at[place, h],
            device_id=(1 - section, group_device(jnp.where(low, 2, 1))), device_id_type=MESH)

    def hop_arrival(place, h):
        return pltpu.make_async_remote_copy(
            second.at[mine, rows_of(h)], hop.at[place, rows_of(h)], s_send.at[1, h], h_recv.at[place, h],
            device_id=(1 - section, group_device(peer(2 + place))), device_id_type=MESH)

    def hop_on(place, h, target):
        device = seq if target == 0 else group_device(peer(1))
        return pltpu.make_async_remote_copy(
            hop.at[place, rows_of(h)], second.at[peer(2 + place), rows_of(h)],
            h_send.at[place, h, target], s_recv.at[2 + place, h],
            device_id=(1 - section, device), device_id_type=MESH)

    def pass_second():
        @pl.when(middle)
        def _():
            for place in range(2):
                for h in range(2):
                    hop_arrival(place, h).wait_recv()
                    hop_on(place, h, 1).start()
                    hop_on(place, h, 0).start()

    def second_arrival(step, h):
        return pltpu.make_async_remote_copy(
            second.at[mine, rows_of(h)], second.at[peer(step), rows_of(h)], s_send.at[0, h], s_recv.at[step, h],
            device_id=(section, group_device(peer(step))), device_id_type=MESH)

    def partial_copy(step, h):
        place = 1 if step == 1 else 2 + lax.rem(mine, 2)
        return pltpu.make_async_remote_copy(
            leaving.at[step, rows_of(h)], landing.at[place, rows_of(h)], p_send.at[step, h], p_recv.at[place, h],
            device_id=(section, group_device(peer(step))), device_id_type=MESH)

    def partial_arrival(place, h):
        return pltpu.make_async_remote_copy(
            leaving.at[place, rows_of(h)], landing.at[place, rows_of(h)], p_send.at[place, h], p_recv.at[place, h],
            device_id=(section, group_device(peer(1))), device_id_type=MESH)

    if plane:
        @pl.when(section == 0)
        def _():
            passed(0).start()
            passed(1).start()
            direct(1, 1).start()
            direct(2, 0).start()

        @pl.when(section == 1)
        def _():
            for which in range(2):
                passed(which).wait_recv()
                for target in (1, 0):
                    passed_on(which, target).start()
            for which in range(2):
                for target in (1, 0):
                    passed_on(which, target).wait_send()
            direct(1, 0).start()
            direct(2, 1).start()
            direct(1, 1).start()
            direct(2, 0).start()
            pass_second()
            for which in range(2):
                landed(1 + which, which).wait_recv()
                onward(which).start()
    else:
        @pl.when(section == 1)
        def _():
            pass_second()
            pl.semaphore_wait(go, 1)

        def send_weights(step, carry):
            weight_copies(step, 0).start()
            weight_copies(step, 1).start()
            return carry

        each(send_weights)

    def await_half(slot, h):
        exists = beside(slot)[0]

        @pl.when(exists)
        def _():
            arrival(slot, h).wait_recv()

        @pl.when(jnp.logical_not(exists))
        def _():
            around[slot, HALF * h:HALF * h + HALF] = jnp.zeros((HALF, width), jnp.bfloat16)

    @pl.when(section == 1)
    def _():
        for h in range(2):
            arrival(4, h).wait_recv()

    entries = ids[...]
    listed = lax.broadcasted_iota(jnp.int32, entries.shape, 1) < count[...]
    flags = []
    for slot in ORDER:
        exists, device = beside(slot)
        wanted = jnp.where(exists, device, jnp.int32(-1))
        hit = jnp.where(listed & (entries == wanted), 1.0, 0.0)
        flags.append(jnp.broadcast_to(jnp.max(hit, axis=1, keepdims=True), (1, BLK)))
    live_row = jnp.concatenate(flags, axis=1)

    normed[pl.ds(0, BLK)] = normalise(around[4].astype(jnp.float32), gain_row)
    locals_[0].wait()

    score_scale = 1.0 / math.sqrt(width // HEADS)
    product = jnp.dot(normed[pl.ds(0, BLK)], wq[...], preferred_element_type=jnp.float32)
    queries[...] = (product.astype(jnp.bfloat16).astype(jnp.float32) * score_scale).astype(jnp.bfloat16)
    locals_[1].wait()
    locals_[2].wait()

    def project(start, count):
        here, there = pl.ds(0, count * BLK), pl.ds(start * BLK, count * BLK)
        keys[there] = jnp.dot(normed[here], wk[...], preferred_element_type=jnp.float32).astype(jnp.bfloat16)
        values[there] = jnp.dot(normed[here], wv[...], preferred_element_type=jnp.float32).astype(jnp.bfloat16)

    project(0, 1)
    for h in range(2):
        for side in range(2):
            await_half(3 + 2 * side, h)
            for index in (side, side + 2):
                @pl.when(relay(index, h)[0])
                def _():
                    relay(index, h)[1].start()
    def gather(first):
        for place in range(first, first + 4):
            slot = ORDER[place]
            if slot not in (3, 5):
                for h in range(2):
                    await_half(slot, h)
            normed[pl.ds((place - first) * BLK, BLK)] = normalise(around[slot].astype(jnp.float32), gain_row)
        project(first, 4)

    first_half = lax.broadcasted_iota(jnp.int32, (BLK, 128), 1) < 64

    def score(at, there):
        q = queries[:, at]
        zero = jnp.zeros_like(q)
        both = jnp.concatenate([jnp.where(first_half, q, zero), jnp.where(first_half, zero, q)], axis=0)
        scores = lax.dot_general(both, keys[there, at], NT, preferred_element_type=jnp.float32)
        return jnp.where(live_row[:, there] > 0.0, scores, -jnp.inf)

    def weigh(scores, top, at, there):
        ones = jnp.ones((scores.shape[1], 128), jnp.bfloat16)
        return jnp.dot(
            jnp.exp(scores - top).astype(jnp.bfloat16), jnp.concatenate([values[there, at], ones], axis=1),
            preferred_element_type=jnp.float32)

    near, far = slice(0, 5 * BLK), slice(5 * BLK, 9 * BLK)

    def near_pair(pair, carry):
        at = pl.ds(pl.multiple_of(pair * 128, 128), 128)
        scores = score(at, near)
        top = jnp.max(scores, axis=-1, keepdims=True)
        near_sum[pair] = weigh(scores, top, at, near)
        near_top[pair] = jnp.broadcast_to(top, (2 * BLK, 128))
        return carry

    def far_pair(pair, carry):
        at = pl.ds(pl.multiple_of(pair * 128, 128), 128)
        scores = score(at, far)
        before = near_top[pair]
        top = jnp.maximum(before, jnp.max(scores, axis=-1, keepdims=True))
        kept = jnp.exp(before - top)
        product = near_sum[pair] * jnp.concatenate([kept, kept], axis=1) + weigh(scores, top[:, :1], at, far)
        product = product[:, :128] / product[:, 128:]
        mixed[:, at] = jnp.where(first_half, product[:BLK], product[BLK:]).astype(jnp.bfloat16)
        return carry

    gather(1)
    lax.fori_loop(0, pairs, near_pair, 0, unroll=8)
    gather(5)
    lax.fori_loop(0, pairs, far_pair, 0, unroll=8)
    locals_[3].wait()
    product = jnp.dot(mixed[...], wo[...], preferred_element_type=jnp.float32)
    attended[...] = (around[4].astype(jnp.float32) + product).astype(jnp.bfloat16)
    second[mine] = normalise(attended[...].astype(jnp.float32), second_gain[...])

    for h in range(2):
        hop_copy(h).start()
    for h in range(2):
        second_copy(h).start()

    locals_[4].wait()
    locals_[5].wait()

    if plane:
        for bits in (1, 2, 3):
            for which in range(2):
                @pl.when((section == 0) | (bits != 1 + which))
                def _():
                    landed(bits, which).wait_recv()
    else:
        def await_weights(step, carry):
            weight_arrival(step, 0).wait_recv()
            weight_arrival(step, 1).wait_recv()
            return carry

        each(await_weights)

        @pl.when(section == 0)
        def _():
            pl.semaphore_signal(go, inc=1, device_id=(1, seq), device_id_type=MESH)

    for step in range(GROUP):
        if step:
            for h in range(2):
                second_arrival(step, h).wait_recv()
        raised = lax.dot_general(second[peer(step)], up[...], NT, preferred_element_type=jnp.float32)
        hidden[...] = jax.nn.gelu(raised, approximate=True).astype(jnp.bfloat16)
        product = jnp.dot(hidden[...], down[...], preferred_element_type=jnp.float32)
        if step:
            leaving[step] = product.astype(jnp.bfloat16)
            for h in range(2):
                partial_copy(step, h).start()
        else:
            total[...] = product

    for h in range(2):
        at = slice(HALF * h, HALF * h + HALF)
        gathered = attended[at].astype(jnp.float32) + total[at]
        for step in range(1, GROUP):
            partial_arrival(step, h).wait_recv()
            gathered = gathered + landing[step, at].astype(jnp.float32)
        result = gathered.astype(jnp.bfloat16)
        finished[at] = result
        out[0, 0, at] = result

        @pl.when(section == 0)
        def _():
            spread(result_copy, h)
            result_copy(4, h).start()

    @pl.when(section == 0)
    def _():
        for slot in (4, 3, 5, 1, 7):
            @pl.when(beside(slot)[0])
            def _():
                for h in range(2):
                    result_copy(slot, h).wait_send()
                    if slot != 4:
                        token_copy(slot, h).wait_send()

    for index in range(4):
        @pl.when(relay(index, 0)[0])
        def _():
            for h in range(2):
                relay(index, h)[1].wait_send()

    @pl.when(section == 0)
    def _():
        pass_second()

    for h in range(2):
        second_copy(h).wait_send()
        hop_copy(h).wait_send()

    @pl.when(middle)
    def _():
        for place in range(2):
            for h in range(2):
                for target in range(2):
                    hop_on(place, h, target).wait_send()

    for step in range(1, GROUP):
        for h in range(2):
            partial_copy(step, h).wait_send()


    if plane:
        direct(1, 1).wait_send()
        direct(2, 0).wait_send()

        @pl.when(section == 0)
        def _():
            passed(0).wait_send()
            passed(1).wait_send()

        @pl.when(section == 1)
        def _():
            for which in range(2):
                direct(1 + which, which).wait_send()
                onward(which).wait_send()
    else:
        def drain(step, carry):
            weight_copies(step, 0).wait_send()
            weight_copies(step, 1).wait_send()
            return carry

        each(drain)


def solution(mesh):
    n = mesh.shape["seq"]

    def local(tokens, ids, count, w_query, w_key, w_value, w_out, gain, w_up, w_down, second_gain):
        width = tokens.shape[-1]
        held = w_up.shape[1] * n // GROUP
        members = n // GROUP
        bf16, f32 = jnp.bfloat16, jnp.float32
        any_ = pl.BlockSpec(memory_space=pltpu.HBM)
        vmem = pl.BlockSpec(memory_space=pltpu.VMEM)
        dma = pltpu.SemaphoreType.DMA
        return pl.pallas_call(
            functools.partial(kernel, n),
            out_shape=pltpu.VMEM((1,) + tokens.shape, bf16),
            in_specs=[vmem, vmem, any_, any_, any_, any_, any_, vmem, any_, any_, vmem],
            out_specs=vmem,
            scratch_shapes=[
                pltpu.VMEM((9, BLK, width), bf16),
                pltpu.VMEM((4 * BLK, width), bf16),
                pltpu.VMEM((BLK, width), bf16),
                pltpu.VMEM((9 * BLK, width), bf16),
                pltpu.VMEM((9 * BLK, width), bf16),
                pltpu.VMEM((BLK, width), bf16),
                pltpu.VMEM((BLK, width), bf16),
                pltpu.VMEM((GROUP, BLK, width), bf16),
                pltpu.VMEM((BLK, held), bf16),
                pltpu.VMEM((BLK, width), f32),
                pltpu.VMEM((GROUP, BLK, width), bf16),
                pltpu.VMEM((GROUP, BLK, width), bf16),
                pltpu.VMEM((BLK, width), bf16),
                pltpu.VMEM((width, width), bf16),
                pltpu.VMEM((width, width), bf16),
                pltpu.VMEM((width, width), bf16),
                pltpu.VMEM((width, width), bf16),
                pltpu.VMEM((held, width), bf16),
                pltpu.VMEM((held, width), bf16),
                pltpu.VMEM((w_up.shape[1], width), bf16),
                pltpu.VMEM((w_up.shape[1], width), bf16),
                pltpu.VMEM((HEADS // 2, 2 * BLK, 256), f32),
                pltpu.VMEM((HEADS // 2, 2 * BLK, 128), f32),
                pltpu.VMEM((2, BLK, width), bf16),
                dma((7,)),
                dma((9, 2)),
                dma((9, 2)),
                dma((9, 2)),
                dma((2 * members,)),
                dma((2 * members,)),
                dma((2, 2)),
                dma((GROUP, 2)),
                dma((GROUP, 2)),
                dma((GROUP, 2)),
                pltpu.SemaphoreType.REGULAR,
                dma((4, 2)),
                dma((6,)),
                dma((2,)),
                dma((2, 2, 2)),
                dma((2, 2)),
            ],
            compiler_params=pltpu.CompilerParams(
                collective_id=0, has_side_effects=True, vmem_limit_bytes=56 * 1024 * 1024),
        )(ids, count.reshape(1, 1), tokens, w_query, w_key, w_value, w_out, gain, w_up, w_down, second_gain)

    in_specs = (
        P(None, "seq", None),
        P("seq", None),
        P("seq"),
        P("section", None, None),
        P("section", None, None),
        P("section", None, None),
        P("section", None, None),
        P("section", None),
        P("section", "seq", None),
        P("section", "seq", None),
        P("section", None),
    )
    return jax.shard_map(
        local, mesh=mesh, in_specs=in_specs, out_specs=P("section", None, "seq", None), check_vma=False)
```

```python
import functools
import math

import jax
import jax.numpy as jnp
from jax import lax
from jax.experimental import pallas as pl
from jax.experimental.pallas import tpu as pltpu
from jax.sharding import PartitionSpec as P

HEADS = 16
BLK = 128
ROW = 4
GROUP = 4
HALF = BLK // 2
ORDER = (4, 3, 5, 1, 7, 0, 2, 6, 8)
MESH = pl.DeviceIdType.MESH
NT = (((1,), (1,)), ((), ()))


def normalise(widened, gain):
    mean = jnp.mean(widened * widened, axis=-1, keepdims=True)
    return (widened * lax.rsqrt(mean + 1e-05) * gain).astype(jnp.bfloat16)


def kernel(
    n, ids, count, tokens, w_query, w_key, w_value, w_out, gain, w_up, w_down, second_gain,
    out,
    around, normed, queries, keys, values, mixed, attended, second, hidden, total, leaving,
    landing, finished, wq, wk, wv, wo, up, down, pass_up, pass_down, near_sum, near_top, hop,
    local_sem, x_send, x_recv, o_send, w_send, w_recv, s_send, s_recv, p_send, p_recv, go, f_send,
    r_send, r_recv, h_send, h_recv,
):
    section, seq = lax.axis_index("section"), lax.axis_index("seq")
    row, col = lax.div(seq, ROW), lax.rem(seq, ROW)
    rows = n // ROW
    width = wq.shape[0]
    units = w_up.shape[1]
    mine = lax.rem(row, GROUP)
    members = n // GROUP
    member = lax.div(row, GROUP) * ROW + col
    pairs = HEADS // 2
    plane = members == 4

    def local(src, dst, index):
        return pltpu.make_async_copy(src, dst, local_sem.at[index])

    own_up = pl.ds(pl.multiple_of(member * units, units), units)
    locals_ = [
        local(w_query.at[0], wq, 0),
        local(w_key.at[0], wk, 1),
        local(w_value.at[0], wv, 2),
        local(w_out.at[0], wo, 3),
        local(w_up.at[0], up.at[own_up], 4),
        local(w_down.at[0], down.at[own_up], 5),
    ]
    own_tokens = local(tokens.at[0], around.at[4], 6)

    @pl.when(section == 0)
    def _():
        own_tokens.start()

    for copy in locals_:
        copy.start()

    def beside(slot):
        dr, dc = slot // 3 - 1, slot % 3 - 1
        exists = (row + dr >= 0) & (row + dr < rows) & (col + dc >= 0) & (col + dc < ROW)
        return exists, jnp.clip(row + dr, 0, rows - 1) * ROW + jnp.clip(col + dc, 0, ROW - 1)

    def member_device(place):
        return (lax.div(place, ROW) * GROUP + mine) * ROW + lax.rem(place, ROW)

    def group_device(index):
        return (lax.div(row, GROUP) * GROUP + index) * ROW + col

    barrier = pltpu.get_barrier_semaphore()

    def greet(device):
        for side in range(2):
            pl.semaphore_signal(barrier, inc=1, device_id=(side, device), device_id_type=MESH)

    def greet_member(step, carry):
        greet(member_device(lax.rem(member + step, members)))
        return carry

    lax.fori_loop(1, members, greet_member, 0)
    for step in range(1, GROUP):
        greet(group_device(lax.rem(mine + step, GROUP)))
    pl.semaphore_signal(barrier, inc=1, device_id=(1 - section, seq), device_id_type=MESH)
    expected = 2 * (members - 1) + 2 * (GROUP - 1) + 1
    if rows > GROUP:
        for slot in (1, 3, 5, 7):
            @pl.when(beside(slot)[0])
            def _():
                greet(beside(slot)[1])
            expected = expected + 2 * beside(slot)[0].astype(jnp.int32)

    gain_row = gain[...]

    @pl.when(section == 0)
    def _():
        own_tokens.wait()

    pl.semaphore_wait(barrier, expected)

    def half(slot, h):
        return around.at[slot, pl.ds(HALF * h, HALF)]

    def token_copy(slot, h):
        device = beside(slot)[1]
        return pltpu.make_async_remote_copy(
            half(4, h), half(8 - slot, h), x_send.at[slot, h], x_recv.at[8 - slot, h],
            device_id=(section, device), device_id_type=MESH)

    def result_copy(slot, h):
        device = beside(slot)[1]
        return pltpu.make_async_remote_copy(
            finished.at[pl.ds(HALF * h, HALF)], half(8 - slot, h), o_send.at[slot, h], x_recv.at[8 - slot, h],
            device_id=(1, device), device_id_type=MESH)

    def relay(index, h):
        side, up_or_down = index % 2 * 2, index // 2 * 2
        device = beside(3 * up_or_down + 1)[1]
        slot = 3 * (2 - up_or_down) + side
        exists = beside(3 + side)[0] & beside(3 * up_or_down + 1)[0]
        return exists, pltpu.make_async_remote_copy(
            half(3 + side, h), half(slot, h), f_send.at[index, h], x_recv.at[slot, h],
            device_id=(section, device), device_id_type=MESH)

    def arrival(slot, h):
        return pltpu.make_async_remote_copy(
            finished.at[pl.ds(HALF * h, HALF)], half(slot, h), o_send.at[slot, h], x_recv.at[slot, h],
            device_id=(section, seq), device_id_type=MESH)

    def spread(copy, h):
        right = col < ROW // 2
        for slot, when in ((5, right), (3, col >= ROW // 2), (1, True), (7, True), (3, right), (5, col >= ROW // 2)):
            @pl.when(when & beside(slot)[0])
            def _():
                copy(slot, h).start()

    def shard(place):
        return pl.ds(pl.multiple_of(place * units, units), units)

    def weight_copies(step, which):
        device = member_device(lax.rem(member + step, members))
        src, dst = (w_up, up) if which == 0 else (w_down, down)
        return pltpu.make_async_remote_copy(
            src.at[0], dst.at[own_up], w_send.at[2 * step + which], w_recv.at[2 * step + which],
            device_id=(section, device), device_id_type=MESH)

    def weight_arrival(step, which):
        there = shard(lax.rem(member + members - step, members))
        src, dst = (w_up, up) if which == 0 else (w_down, down)
        return pltpu.make_async_remote_copy(
            src.at[0], dst.at[there], w_send.at[2 * step + which], w_recv.at[2 * step + which],
            device_id=(section, seq), device_id_type=MESH)

    def across(bits):
        base = lax.rem(member, 4)
        low, high = lax.rem(base, 2), lax.div(base, 2)
        if bits % 2:
            low = 1 - low
        if bits // 2:
            high = 1 - high
        return 2 * high + low

    def direct(bits, which):
        src, dst = (w_up, up) if which == 0 else (w_down, down)
        return pltpu.make_async_remote_copy(
            src.at[0], dst.at[own_up], w_send.at[2 * bits + which], w_recv.at[2 * bits + which],
            device_id=(section, member_device(across(bits))), device_id_type=MESH)

    def landed(bits, which):
        src, dst = (w_up, up) if which == 0 else (w_down, down)
        return pltpu.make_async_remote_copy(
            src.at[0], dst.at[shard(across(bits))], w_send.at[2 * bits + which], w_recv.at[2 * bits + which],
            device_id=(section, member_device(across(bits))), device_id_type=MESH)

    def onward(which):
        dst = up if which == 0 else down
        there = shard(across(1 + which))
        return pltpu.make_async_remote_copy(
            dst.at[there], dst.at[there], w_send.at[6 + which], w_recv.at[6 + which],
            device_id=(section, member_device(across(2 - which))), device_id_type=MESH)

    def passed(which):
        src, dst = (w_up, pass_up) if which == 0 else (w_down, pass_down)
        return pltpu.make_async_remote_copy(
            src.at[0], dst, r_send.at[which], r_recv.at[which],
            device_id=(1, member_device(across(1 + which))), device_id_type=MESH)

    def passed_on(which, target):
        src, dst = (pass_up, up) if which == 0 else (pass_down, down)
        bits = 1 + which
        device = seq if target == 0 else member_device(across(2 - which))
        index = 2 * bits + which if target == 0 else 6 + which
        return pltpu.make_async_remote_copy(
            src, dst.at[shard(across(bits))], r_send.at[2 + 2 * target + which], w_recv.at[index],
            device_id=(0, device), device_id_type=MESH)

    def each(body):
        if members > 8:
            lax.fori_loop(1, members, body, 0)
        else:
            for step in range(1, members):
                body(step, 0)

    @pl.when(section == 0)
    def _():
        for h in range(2):
            spread(token_copy, h)

    low = mine < 2
    middle = (mine == 1) | (mine == 2)

    def peer(step):
        if step < 2:
            return mine if step == 0 else mine + 1 - 2 * lax.rem(mine, 2)
        return jnp.where(low, step, 3 - step)

    def rows_of(h):
        return pl.ds(HALF * h, HALF)

    def second_copy(h):
        return pltpu.make_async_remote_copy(
            second.at[mine, rows_of(h)], second.at[mine, rows_of(h)], s_send.at[0, h], s_recv.at[1, h],
            device_id=(section, group_device(peer(1))), device_id_type=MESH)

    def hop_copy(h):
        place = jnp.where(middle, 0, 1)
        return pltpu.make_async_remote_copy(
            second.at[mine, rows_of(h)], hop.at[place, rows_of(h)], s_send.at[1, h], h_recv.at[place, h],
            device_id=(1 - section, group_device(jnp.where(low, 2, 1))), device_id_type=MESH)

    def hop_arrival(place, h):
        return pltpu.make_async_remote_copy(
            second.at[mine, rows_of(h)], hop.at[place, rows_of(h)], s_send.at[1, h], h_recv.at[place, h],
            device_id=(1 - section, group_device(peer(2 + place))), device_id_type=MESH)

    def hop_on(place, h, target):
        device = seq if target == 0 else group_device(peer(1))
        return pltpu.make_async_remote_copy(
            hop.at[place, rows_of(h)], second.at[peer(2 + place), rows_of(h)],
            h_send.at[place, h, target], s_recv.at[2 + place, h],
            device_id=(1 - section, device), device_id_type=MESH)

    def pass_second():
        @pl.when(middle)
        def _():
            for place in range(2):
                for h in range(2):
                    hop_arrival(place, h).wait_recv()
                    hop_on(place, h, 1).start()
                    hop_on(place, h, 0).start()

    def second_arrival(step, h):
        return pltpu.make_async_remote_copy(
            second.at[mine, rows_of(h)], second.at[peer(step), rows_of(h)], s_send.at[0, h], s_recv.at[step, h],
            device_id=(section, group_device(peer(step))), device_id_type=MESH)

    def partial_copy(step, h):
        place = 1 if step == 1 else 2 + lax.rem(mine, 2)
        return pltpu.make_async_remote_copy(
            leaving.at[step, rows_of(h)], landing.at[place, rows_of(h)], p_send.at[step, h], p_recv.at[place, h],
            device_id=(section, group_device(peer(step))), device_id_type=MESH)

    def partial_arrival(place, h):
        return pltpu.make_async_remote_copy(
            leaving.at[place, rows_of(h)], landing.at[place, rows_of(h)], p_send.at[place, h], p_recv.at[place, h],
            device_id=(section, group_device(peer(1))), device_id_type=MESH)

    if plane:
        @pl.when(section == 0)
        def _():
            passed(0).start()
            passed(1).start()
            direct(1, 1).start()
            direct(2, 0).start()

        @pl.when(section == 1)
        def _():
            for which in range(2):
                passed(which).wait_recv()
                for target in (1, 0):
                    passed_on(which, target).start()
            for which in range(2):
                for target in (1, 0):
                    passed_on(which, target).wait_send()
            direct(1, 0).start()
            direct(2, 1).start()
            direct(1, 1).start()
            direct(2, 0).start()
            pass_second()
            for which in range(2):
                landed(1 + which, which).wait_recv()
                onward(which).start()
    else:
        @pl.when(section == 1)
        def _():
            pass_second()
            pl.semaphore_wait(go, 1)

        def send_weights(step, carry):
            weight_copies(step, 0).start()
            weight_copies(step, 1).start()
            return carry

        each(send_weights)

    def await_half(slot, h):
        exists = beside(slot)[0]

        @pl.when(exists)
        def _():
            arrival(slot, h).wait_recv()

        @pl.when(jnp.logical_not(exists))
        def _():
            around[slot, HALF * h:HALF * h + HALF] = jnp.zeros((HALF, width), jnp.bfloat16)

    @pl.when(section == 1)
    def _():
        for h in range(2):
            arrival(4, h).wait_recv()

    entries = ids[...]
    listed = lax.broadcasted_iota(jnp.int32, entries.shape, 1) < count[...]
    flags = []
    for slot in ORDER:
        exists, device = beside(slot)
        wanted = jnp.where(exists, device, jnp.int32(-1))
        hit = jnp.where(listed & (entries == wanted), 1.0, 0.0)
        flags.append(jnp.broadcast_to(jnp.max(hit, axis=1, keepdims=True), (1, BLK)))
    live_row = jnp.concatenate(flags, axis=1)

    normed[pl.ds(0, BLK)] = normalise(around[4].astype(jnp.float32), gain_row)
    locals_[0].wait()

    score_scale = 1.0 / math.sqrt(width // HEADS)
    product = jnp.dot(normed[pl.ds(0, BLK)], wq[...], preferred_element_type=jnp.float32)
    queries[...] = (product.astype(jnp.bfloat16).astype(jnp.float32) * score_scale).astype(jnp.bfloat16)
    locals_[1].wait()
    locals_[2].wait()

    def project(start, count):
        here, there = pl.ds(0, count * BLK), pl.ds(start * BLK, count * BLK)
        keys[there] = jnp.dot(normed[here], wk[...], preferred_element_type=jnp.float32).astype(jnp.bfloat16)
        values[there] = jnp.dot(normed[here], wv[...], preferred_element_type=jnp.float32).astype(jnp.bfloat16)

    project(0, 1)
    for h in range(2):
        for side in range(2):
            await_half(3 + 2 * side, h)
            for index in (side, side + 2):
                @pl.when(relay(index, h)[0])
                def _():
                    relay(index, h)[1].start()
    def gather(first):
        for place in range(first, first + 4):
            slot = ORDER[place]
            if slot not in (3, 5):
                for h in range(2):
                    await_half(slot, h)
            normed[pl.ds((place - first) * BLK, BLK)] = normalise(around[slot].astype(jnp.float32), gain_row)
        project(first, 4)

    first_half = lax.broadcasted_iota(jnp.int32, (BLK, 128), 1) < 64

    def score(at, there):
        q = queries[:, at]
        zero = jnp.zeros_like(q)
        both = jnp.concatenate([jnp.where(first_half, q, zero), jnp.where(first_half, zero, q)], axis=0)
        scores = lax.dot_general(both, keys[there, at], NT, preferred_element_type=jnp.float32)
        return jnp.where(live_row[:, there] > 0.0, scores, -jnp.inf)

    def weigh(scores, top, at, there):
        ones = jnp.ones((scores.shape[1], 128), jnp.bfloat16)
        return jnp.dot(
            jnp.exp(scores - top).astype(jnp.bfloat16), jnp.concatenate([values[there, at], ones], axis=1),
            preferred_element_type=jnp.float32)

    near, far = slice(0, 5 * BLK), slice(5 * BLK, 9 * BLK)

    def near_pair(pair, carry):
        at = pl.ds(pl.multiple_of(pair * 128, 128), 128)
        scores = score(at, near)
        top = jnp.max(scores, axis=-1, keepdims=True)
        near_sum[pair] = weigh(scores, top, at, near)
        near_top[pair] = jnp.broadcast_to(top, (2 * BLK, 128))
        return carry

    def far_pair(pair, carry):
        at = pl.ds(pl.multiple_of(pair * 128, 128), 128)
        scores = score(at, far)
        before = near_top[pair]
        top = jnp.maximum(before, jnp.max(scores, axis=-1, keepdims=True))
        kept = jnp.exp(before - top)
        product = near_sum[pair] * jnp.concatenate([kept, kept], axis=1) + weigh(scores, top[:, :1], at, far)
        product = product[:, :128] / product[:, 128:]
        mixed[:, at] = jnp.where(first_half, product[:BLK], product[BLK:]).astype(jnp.bfloat16)
        return carry

    gather(1)
    lax.fori_loop(0, pairs, near_pair, 0, unroll=8)
    gather(5)
    lax.fori_loop(0, pairs, far_pair, 0, unroll=8)
    locals_[3].wait()
    product = jnp.dot(mixed[...], wo[...], preferred_element_type=jnp.float32)
    attended[...] = (around[4].astype(jnp.float32) + product).astype(jnp.bfloat16)
    second[mine] = normalise(attended[...].astype(jnp.float32), second_gain[...])

    for h in range(2):
        second_copy(h).start()
    for h in range(2):
        hop_copy(h).start()

    locals_[4].wait()
    locals_[5].wait()

    if plane:
        for bits in (1, 2, 3):
            for which in range(2):
                @pl.when((section == 0) | (bits != 1 + which))
                def _():
                    landed(bits, which).wait_recv()
    else:
        def await_weights(step, carry):
            weight_arrival(step, 0).wait_recv()
            weight_arrival(step, 1).wait_recv()
            return carry

        each(await_weights)

        @pl.when(section == 0)
        def _():
            pl.semaphore_signal(go, inc=1, device_id=(1, seq), device_id_type=MESH)

    for step in range(GROUP):
        if step:
            for h in range(2):
                second_arrival(step, h).wait_recv()
        raised = lax.dot_general(second[peer(step)], up[...], NT, preferred_element_type=jnp.float32)
        hidden[...] = jax.nn.gelu(raised, approximate=True).astype(jnp.bfloat16)
        product = jnp.dot(hidden[...], down[...], preferred_element_type=jnp.float32)
        if step:
            leaving[step] = product.astype(jnp.bfloat16)
            for h in range(2):
                partial_copy(step, h).start()
        else:
            total[...] = product

    for h in range(2):
        at = slice(HALF * h, HALF * h + HALF)
        gathered = attended[at].astype(jnp.float32) + total[at]
        for step in range(1, GROUP):
            partial_arrival(step, h).wait_recv()
            gathered = gathered + landing[step, at].astype(jnp.float32)
        result = gathered.astype(jnp.bfloat16)
        finished[at] = result
        out[0, 0, at] = result

        @pl.when(section == 0)
        def _():
            spread(result_copy, h)
            result_copy(4, h).start()

    @pl.when(section == 0)
    def _():
        for slot in (4, 3, 5, 1, 7):
            @pl.when(beside(slot)[0])
            def _():
                for h in range(2):
                    result_copy(slot, h).wait_send()
                    if slot != 4:
                        token_copy(slot, h).wait_send()

    for index in range(4):
        @pl.when(relay(index, 0)[0])
        def _():
            for h in range(2):
                relay(index, h)[1].wait_send()

    @pl.when(section == 0)
    def _():
        pass_second()

    for h in range(2):
        second_copy(h).wait_send()
        hop_copy(h).wait_send()

    @pl.when(middle)
    def _():
        for place in range(2):
            for h in range(2):
                for target in range(2):
                    hop_on(place, h, target).wait_send()

    for step in range(1, GROUP):
        for h in range(2):
            partial_copy(step, h).wait_send()


    if plane:
        direct(1, 1).wait_send()
        direct(2, 0).wait_send()

        @pl.when(section == 0)
        def _():
            passed(0).wait_send()
            passed(1).wait_send()

        @pl.when(section == 1)
        def _():
            for which in range(2):
                direct(1 + which, which).wait_send()
                onward(which).wait_send()
    else:
        def drain(step, carry):
            weight_copies(step, 0).wait_send()
            weight_copies(step, 1).wait_send()
            return carry

        each(drain)


def solution(mesh):
    n = mesh.shape["seq"]

    def local(tokens, ids, count, w_query, w_key, w_value, w_out, gain, w_up, w_down, second_gain):
        width = tokens.shape[-1]
        held = w_up.shape[1] * n // GROUP
        members = n // GROUP
        bf16, f32 = jnp.bfloat16, jnp.float32
        any_ = pl.BlockSpec(memory_space=pltpu.HBM)
        vmem = pl.BlockSpec(memory_space=pltpu.VMEM)
        dma = pltpu.SemaphoreType.DMA
        return pl.pallas_call(
            functools.partial(kernel, n),
            out_shape=pltpu.VMEM((1,) + tokens.shape, bf16),
            in_specs=[vmem, vmem, any_, any_, any_, any_, any_, vmem, any_, any_, vmem],
            out_specs=vmem,
            scratch_shapes=[
                pltpu.VMEM((9, BLK, width), bf16),
                pltpu.VMEM((4 * BLK, width), bf16),
                pltpu.VMEM((BLK, width), bf16),
                pltpu.VMEM((9 * BLK, width), bf16),
                pltpu.VMEM((9 * BLK, width), bf16),
                pltpu.VMEM((BLK, width), bf16),
                pltpu.VMEM((BLK, width), bf16),
                pltpu.VMEM((GROUP, BLK, width), bf16),
                pltpu.VMEM((BLK, held), bf16),
                pltpu.VMEM((BLK, width), f32),
                pltpu.VMEM((GROUP, BLK, width), bf16),
                pltpu.VMEM((GROUP, BLK, width), bf16),
                pltpu.VMEM((BLK, width), bf16),
                pltpu.VMEM((width, width), bf16),
                pltpu.VMEM((width, width), bf16),
                pltpu.VMEM((width, width), bf16),
                pltpu.VMEM((width, width), bf16),
                pltpu.VMEM((held, width), bf16),
                pltpu.VMEM((held, width), bf16),
                pltpu.VMEM((w_up.shape[1], width), bf16),
                pltpu.VMEM((w_up.shape[1], width), bf16),
                pltpu.VMEM((HEADS // 2, 2 * BLK, 256), f32),
                pltpu.VMEM((HEADS // 2, 2 * BLK, 128), f32),
                pltpu.VMEM((2, BLK, width), bf16),
                dma((7,)),
                dma((9, 2)),
                dma((9, 2)),
                dma((9, 2)),
                dma((2 * members,)),
                dma((2 * members,)),
                dma((2, 2)),
                dma((GROUP, 2)),
                dma((GROUP, 2)),
                dma((GROUP, 2)),
                pltpu.SemaphoreType.REGULAR,
                dma((4, 2)),
                dma((6,)),
                dma((2,)),
                dma((2, 2, 2)),
                dma((2, 2)),
            ],
            compiler_params=pltpu.CompilerParams(
                collective_id=0, has_side_effects=True, vmem_limit_bytes=56 * 1024 * 1024),
        )(ids, count.reshape(1, 1), tokens, w_query, w_key, w_value, w_out, gain, w_up, w_down, second_gain)

    in_specs = (
        P(None, "seq", None),
        P("seq", None),
        P("seq"),
        P("section", None, None),
        P("section", None, None),
        P("section", None, None),
        P("section", None, None),
        P("section", None),
        P("section", "seq", None),
        P("section", "seq", None),
        P("section", None),
    )
    return jax.shard_map(
        local, mesh=mesh, in_specs=in_specs, out_specs=P("section", None, "seq", None), check_vma=False)
```
